32 devices in a mesh: freq: 2 (over y), harm: 4 (over z), wall: 4 (over x, core).
Axes of the slice: x: 2, y: 2, z: 4, core: 2. Of those that a mesh axis runs over, the one named last changes fastest.
Arguments:
- sketch: bfloat16 [32, 1024, 128], P(('freq', 'harm'), 'wall'), parts along dimension 0, may hold values from -48 to 48
- inverse_blocks: bfloat16 [32, 1024, 1024], P(('freq', 'harm'), 'wall'), parts along dimension 0, may hold values from -0.1875 to 0.1875
- couple_up: bfloat16 [8, 1024, 1024], P('freq', 'wall'), parts along dimension 0, may hold values from -0.03125 to 0.03125
- couple_down: bfloat16 [8, 1024, 1024], P('freq', 'wall'), parts along dimension 0, may hold values from -0.03125 to 0.03125
- strip_harmonics: int32 [8], P('freq'), parts along dimension 0, may hold values from 0 to 3
Outputs:
- basis: float32 [32, 1024, 128], P(('freq', 'harm'), 'wall'), parts along dimension 0
- triangle: float32 [256, 128], P('freq'), parts along dimension 0
The draws below stay inside these ranges and needn't reach their ends.
There are 2 independent parts, one for each index of `freq`. The reference program is written for one: setup_inputs(seed, part) draws one part's arguments, and reference() takes and returns one part's arrays. A program takes and returns all parts, laid end to end along the dimension named above; each array names one. Nothing has to cross between parts.
Inputs may be any that keep to these rules, and one draw needn't show every extreme that they name: `strip_harmonics`: each entry one of 0 to 3; entries may repeat.
All inputs are finite; a program needn't handle non-finite values.
Results may differ from the reference program's by a relative error of at most 0.0045.
Values may be sent and summed in bfloat16 or wider, within the bound.
No kernel may reach another device: no remote copies, remote signals or barrier semaphores. Data moves between devices by JAX's collectives and lax.ppermute only.
A program may use at most 64 MiB of HBM per device.

```python
import math
import jax
import jax.numpy as jnp
from jax import lax

ROWS = 1024
COLUMNS = 128
BAND = 4
SWEEPS = 3
HARMONICS = 16


def draw_sketch(key, part):
    scale_key = jax.random.fold_in(key, 7101)
    entry_key = jax.random.fold_in(key, 7102)
    levels = jax.random.uniform(scale_key, (HARMONICS, 1, 1), jnp.float32, 0.0, math.log(8.0))
    amplitude = jnp.exp(levels)
    entries = jnp.clip(jax.random.normal(entry_key, (HARMONICS, ROWS, COLUMNS), jnp.float32), -6.0, 6.0)
    return (entries * amplitude).astype(jnp.bfloat16)


def place_ends(drawn, rng, smallest, largest):
    index_at = [jax.random.randint(jax.random.fold_in(rng, axis), (), 0, length) for axis, length in enumerate(drawn.shape)]
    longest = drawn.shape.index(max(drawn.shape))
    next_to = index_at[:longest] + [(index_at[longest] + 1) % drawn.shape[longest]] + index_at[longest + 1:]
    return drawn.at[tuple(index_at)].set(smallest).at[tuple(next_to)].set(largest)


def level_of(own_key, dims, split, smallest, largest):
    gain = 1.0
    for axis_at, shards_of in split:
        heights = jax.random.uniform(jax.random.fold_in(jax.random.fold_in(own_key, 6), axis_at), (shards_of,), jnp.float32, smallest / len(split), largest / len(split))
        gain = gain * jnp.repeat(jnp.exp(heights), dims[axis_at] // shards_of).reshape((-1,) + (1,) * (len(dims) - 1 - axis_at))
    return gain


def gaussian(key, dims, width, reach, split=(), held_as=jnp.bfloat16):
    level = level_of(key, dims, split, -0.22, 0.18) if split else 1.0
    values = jax.random.normal(key, dims, jnp.float32) * width * level
    return jnp.minimum(jnp.maximum(values, -reach), reach).astype(held_as)


def setup_inputs(seed: int = 0, part: int = 0) -> dict:
    splits = jax.random.split(jax.random.key(seed), 6)
    part_keys = jax.random.split(jax.random.fold_in(splits[5], part), 6)
    sketch = draw_sketch(jax.random.fold_in(jax.random.fold_in(splits[5], part), 71), part)
    inverse_blocks = gaussian(part_keys[1], (HARMONICS, ROWS, ROWS), ROWS ** -0.5, 0.1875, ((0, 4), (1, 4)))
    couple_up = gaussian(part_keys[2], (BAND, ROWS, ROWS), (32 * ROWS) ** -0.5, 0.03125, ((1, 4),))
    couple_down = gaussian(part_keys[3], (BAND, ROWS, ROWS), (32 * ROWS) ** -0.5, 0.03125, ((1, 4),))
    strip_harmonics = place_ends(jax.random.randint(part_keys[4], (BAND,), 0, BAND), jax.random.fold_in(part_keys[4], 1), 0, BAND - 1).astype(jnp.int32)
    return {"sketch": sketch, "inverse_blocks": inverse_blocks, "couple_up": couple_up, "couple_down": couple_down, "strip_harmonics": strip_harmonics}


def reference(sketch, inverse_blocks, couple_up, couple_down, strip_harmonics):
    offsets = (strip_harmonics + 1).astype(jnp.int32)
    inverse_wide = inverse_blocks.astype(jnp.float32)
    up_wide = couple_up.astype(jnp.float32)
    down_wide = couple_down.astype(jnp.float32)
    sketch_wide = sketch.astype(jnp.float32)
    positions = jnp.arange(HARMONICS, dtype=jnp.int32)

    def apply_inverse(source):
        return jnp.einsum('hrc,hck->hrk', inverse_wide, source.astype(jnp.float32))
    state = apply_inverse(sketch).astype(jnp.bfloat16)
    sampled = None
    for sweep in range(SWEEPS):
        coupled = jnp.zeros((HARMONICS, ROWS, COLUMNS), jnp.float32)
        state_wide = state.astype(jnp.float32)
        for j in range(BAND):
            below = jnp.take(state_wide, (positions - offsets[j]) % HARMONICS, axis=0)
            above = jnp.take(state_wide, (positions + offsets[j]) % HARMONICS, axis=0)
            coupled = coupled + jnp.einsum('rc,hck->hrk', up_wide[j], below)
            coupled = coupled + jnp.einsum('rc,hck->hrk', down_wide[j], above)
        rhs = (sketch_wide - coupled).astype(jnp.bfloat16)
        result = apply_inverse(rhs)
        if sweep < SWEEPS - 1:
            state = result.astype(jnp.bfloat16)
        else:
            sampled = result
    flat = sampled.reshape(HARMONICS * ROWS, COLUMNS)
    count = HARMONICS * ROWS
    gram = jnp.dot(flat.T.astype(jnp.float32), flat.astype(jnp.float32), precision=lax.Precision.HIGHEST, preferred_element_type=jnp.float32) / count
    lower = jnp.linalg.cholesky(gram)
    basis = jax.scipy.linalg.solve_triangular(lower, flat.T, lower=True).T
    triangle = lower.T
    return (basis.reshape(HARMONICS, ROWS, COLUMNS), triangle)
```

```python
import functools

import jax
import jax.numpy as jnp
from jax import lax
from jax.experimental import pallas as pl
from jax.experimental.pallas import tpu as pltpu
from jax.sharding import PartitionSpec as P

BAND = 4
SWEEPS = 3
F32 = jnp.float32
BF16 = jnp.bfloat16
VMEM = pl.BlockSpec(memory_space=pltpu.VMEM)
SMEM = pl.BlockSpec(memory_space=pltpu.SMEM)


def flip(value, axis, mask):
    return lax.ppermute(value, axis, [(i, i ^ mask) for i in range(lax.axis_size(axis))])


def turn(value, axis, step):
    count = lax.axis_size(axis)
    return lax.ppermute(value, axis, [(i, (i + step) % count) for i in range(count)])


def wall_pieces(own):
    pieces = {0: own}
    bit = lax.axis_size("wall") // 2
    while bit:
        for mask in list(pieces):
            pieces[mask ^ bit] = flip(pieces[mask], "wall", bit)
        bit //= 2
    return [pieces[mask] for mask in range(len(pieces))]


def columns_of(place, mask, rows):
    return pl.ds(pl.multiple_of((place ^ mask) * rows, rows), rows)


def params(mib):
    return pltpu.CompilerParams(vmem_limit_bytes=mib << 20)


def inverse_kernel(shards, with_gram, place_ref, blocks_ref, *refs):
    pieces, outs = refs[:shards], refs[shards:]
    count, rows, width = pieces[0].shape
    place = place_ref[0]
    gram = jnp.zeros((width, width), F32)
    for h in range(count):
        total = jnp.zeros((rows, width), F32)
        for mask in range(shards):
            total += jnp.dot(
                blocks_ref[h, :, columns_of(place, mask, rows)],
                pieces[mask][h],
                preferred_element_type=F32,
            )
        outs[0][h] = total.astype(outs[0].dtype)
        if with_gram:
            gram += lax.dot_general(
                total,
                total,
                (((0,), (0,)), ((), ())),
                precision=lax.Precision.HIGHEST,
                preferred_element_type=F32,
            )
    if with_gram:
        outs[1][...] = gram


def apply_inverse(place, blocks, source, last):
    pieces = wall_pieces(source)
    shape, width = source.shape, source.shape[2]
    out = [jax.ShapeDtypeStruct(shape, F32 if last else BF16)]
    if last:
        out.append(jax.ShapeDtypeStruct((width, width), F32))
    return pl.pallas_call(
        functools.partial(inverse_kernel, len(pieces), last),
        out_shape=out,
        in_specs=[SMEM, VMEM] + [VMEM] * len(pieces),
        out_specs=[VMEM] * len(out),
        compiler_params=params(12),
    )(place, blocks, *pieces)


def couple_kernel(shards, place_ref, strip_ref, up_ref, down_ref, *refs):
    pieces = refs[:shards]
    own_ref, below_ref, above_ref, total = refs[shards:]
    count, rows, width = pieces[0].shape
    place = place_ref[0]
    total[...] = jnp.zeros_like(total)
    wide = [jnp.concatenate([p[h] for h in range(count)], axis=1) for p in pieces]
    for j in range(BAND):
        offset = strip_ref[j] + 1
        for weights, shift in ((up_ref, offset), (down_ref, -offset)):
            part = jnp.zeros((rows, count * width), F32)
            for mask in range(shards):
                part += jnp.dot(
                    weights[j, :, columns_of(place, mask, rows)],
                    wide[mask],
                    preferred_element_type=F32,
                )
            for h in range(count):
                total[BAND + shift + h] += part[:, h * width : (h + 1) * width]
    own_ref[...] = total[BAND : BAND + count]
    below_ref[...] = total[:BAND].astype(below_ref.dtype)
    above_ref[...] = total[BAND + count :].astype(above_ref.dtype)


def couple(place, strips, up, down, state):
    pieces = wall_pieces(state)
    count, rows, width = state.shape
    own, below, above = pl.pallas_call(
        functools.partial(couple_kernel, len(pieces)),
        out_shape=[
            jax.ShapeDtypeStruct((count, rows, width), F32),
            jax.ShapeDtypeStruct((BAND, rows, width), BF16),
            jax.ShapeDtypeStruct((BAND, rows, width), BF16),
        ],
        in_specs=[SMEM, SMEM, VMEM, VMEM] + [VMEM] * len(pieces),
        out_specs=[VMEM] * 3,
        scratch_shapes=[pltpu.VMEM((count + 2 * BAND, rows, width), F32)],
        compiler_params=params(20),
    )(place, strips, up, down, *pieces)
    from_before = turn(above, "harm", 1)
    from_after = turn(below, "harm", -1)
    return own, from_before, from_after


def all_sum(value):
    for axis in ("wall", "harm"):
        bit = 1
        while bit < lax.axis_size(axis):
            value = value + flip(value, axis, bit)
            bit *= 2
    return value


def body(sketch, inverse_blocks, couple_up, couple_down, strip_harmonics):
    count, rows, width = sketch.shape
    place = lax.axis_index("wall").astype(jnp.int32).reshape(1)
    (state,) = apply_inverse(place, inverse_blocks, sketch, False)
    for sweep in range(SWEEPS):
        own, before, after = couple(place, strip_harmonics, couple_up, couple_down, state)
        coupled = own
        if count == BAND:
            coupled = own + before.astype(F32) + after.astype(F32)
        else:
            coupled = coupled.at[:BAND].add(before.astype(F32))
            coupled = coupled.at[count - BAND :].add(after.astype(F32))
        rhs = (sketch.astype(F32) - coupled).astype(BF16)
        if sweep < SWEEPS - 1:
            (state,) = apply_inverse(place, inverse_blocks, rhs, False)
        else:
            sampled, gram = apply_inverse(place, inverse_blocks, rhs, True)
    entries = lax.axis_size("harm") * lax.axis_size("wall") * count * rows
    gram = all_sum(gram) / entries
    lower = jnp.linalg.cholesky(gram)
    flat = sampled.reshape(count * rows, width)
    basis = jax.scipy.linalg.solve_triangular(lower, flat.T, lower=True).T
    return (basis.reshape(count, rows, width), lower.T)


def solution(mesh):
    return jax.shard_map(
        body,
        mesh=mesh,
        in_specs=(
            P(("freq", "harm"), "wall", None),
            P(("freq", "harm"), "wall", None),
            P("freq", "wall", None),
            P("freq", "wall", None),
            P("freq"),
        ),
        out_specs=(P(("freq", "harm"), "wall", None), P("freq", None)),
        check_vma=False,
    )
```

```python
import functools

import jax
import jax.numpy as jnp
from jax import lax
from jax.experimental import pallas as pl
from jax.experimental.pallas import tpu as pltpu
from jax.sharding import PartitionSpec as P

BAND = 4
SWEEPS = 3
SUB = 8
F32 = jnp.float32
BF16 = jnp.bfloat16
VMEM = pl.BlockSpec(memory_space=pltpu.VMEM)
SMEM = pl.BlockSpec(memory_space=pltpu.SMEM)


def flip(value, axis, mask):
    return lax.ppermute(value, axis, [(i, i ^ mask) for i in range(lax.axis_size(axis))])


def turn(value, axis, step):
    count = lax.axis_size(axis)
    return lax.ppermute(value, axis, [(i, (i + step) % count) for i in range(count)])


def wall_pieces(own):
    pieces = {0: own}
    bit = lax.axis_size("wall") // 2
    while bit:
        for mask in list(pieces):
            pieces[mask ^ bit] = flip(pieces[mask], "wall", bit)
        bit //= 2
    return [pieces[mask] for mask in range(len(pieces))]


def columns_of(place, mask, rows):
    return pl.ds(pl.multiple_of((place ^ mask) * rows, rows), rows)


def params(mib):
    return pltpu.CompilerParams(vmem_limit_bytes=mib << 20)


def inverse_kernel(shards, with_gram, place_ref, blocks_ref, *refs):
    pieces, outs = refs[:shards], refs[shards:]
    count, rows, width = pieces[0].shape
    place = place_ref[0]
    gram = jnp.zeros((width, width), F32)
    for h in range(count):
        total = jnp.zeros((rows, width), F32)
        for mask in range(shards):
            total += jnp.dot(
                blocks_ref[h, :, columns_of(place, mask, rows)],
                pieces[mask][h],
                preferred_element_type=F32,
            )
        outs[0][h] = total.astype(outs[0].dtype)
        if with_gram:
            gram += lax.dot_general(
                total,
                total,
                (((0,), (0,)), ((), ())),
                precision=lax.Precision.HIGHEST,
                preferred_element_type=F32,
            )
    if with_gram:
        outs[1][...] = gram


def apply_inverse(place, blocks, source, last):
    pieces = wall_pieces(source)
    shape, width = source.shape, source.shape[2]
    out = [jax.ShapeDtypeStruct(shape, F32 if last else BF16)]
    if last:
        out.append(jax.ShapeDtypeStruct((width, width), F32))
    return pl.pallas_call(
        functools.partial(inverse_kernel, len(pieces), last),
        out_shape=out,
        in_specs=[SMEM, VMEM] + [VMEM] * len(pieces),
        out_specs=[VMEM] * len(out),
        compiler_params=params(12),
    )(place, blocks, *pieces)


def couple_kernel(shards, place_ref, strip_ref, up_ref, down_ref, *refs):
    pieces = refs[:shards]
    own_ref, below_ref, above_ref, total = refs[shards:]
    count, rows, width = pieces[0].shape
    place = place_ref[0]
    total[...] = jnp.zeros_like(total)
    wide = [jnp.concatenate([p[h] for h in range(count)], axis=1) for p in pieces]
    for j in range(BAND):
        offset = strip_ref[j] + 1
        for weights, shift in ((up_ref, offset), (down_ref, -offset)):
            part = jnp.zeros((rows, count * width), F32)
            for mask in range(shards):
                part += jnp.dot(
                    weights[j, :, columns_of(place, mask, rows)],
                    wide[mask],
                    preferred_element_type=F32,
                )
            for h in range(count):
                total[BAND + shift + h] += part[:, h * width : (h + 1) * width]
    own_ref[...] = total[BAND : BAND + count]
    below_ref[...] = total[:BAND].astype(below_ref.dtype)
    above_ref[...] = total[BAND + count :].astype(above_ref.dtype)


def couple(place, strips, up, down, state):
    pieces = wall_pieces(state)
    count, rows, width = state.shape
    own, below, above = pl.pallas_call(
        functools.partial(couple_kernel, len(pieces)),
        out_shape=[
            jax.ShapeDtypeStruct((count, rows, width), F32),
            jax.ShapeDtypeStruct((BAND, rows, width), BF16),
            jax.ShapeDtypeStruct((BAND, rows, width), BF16),
        ],
        in_specs=[SMEM, SMEM, VMEM, VMEM] + [VMEM] * len(pieces),
        out_specs=[VMEM] * 3,
        scratch_shapes=[pltpu.VMEM((count + 2 * BAND, rows, width), F32)],
        compiler_params=params(20),
    )(place, strips, up, down, *pieces)
    from_before = turn(above, "harm", 1)
    from_after = turn(below, "harm", -1)
    return own, from_before, from_after


def all_sum(value):
    for axis in ("wall", "harm"):
        bit = 1
        while bit < lax.axis_size(axis):
            value = value + flip(value, axis, bit)
            bit *= 2
    return value


def spread(row, height):
    return jnp.broadcast_to(row, (height, row.shape[1]))


def factor(gram):
    size = gram.shape[0]
    panels = size // SUB
    level = lax.broadcasted_iota(jnp.int32, (SUB, size), 0)
    lane = lax.broadcasted_iota(jnp.int32, (SUB, size), 1)
    upper = [gram[SUB * p : SUB * (p + 1)] for p in range(panels)]
    inverse = [jnp.where(lane == level + SUB * p, 1.0, 0.0) for p in range(panels)]
    for p in range(panels):
        column = {
            q: [
                jnp.broadcast_to(upper[q][:, SUB * p + j : SUB * p + j + 1], (SUB, size))
                for j in range(SUB)
            ]
            for q in range(p, panels)
        }
        for k in range(SUB):
            scale = lax.rsqrt(spread(column[p][k][k : k + 1], SUB))
            heads = [spread(column[p][j][k : k + 1], SUB) * scale for j in range(k + 1, SUB)]
            row = spread(upper[p][k : k + 1], SUB) * scale
            back = spread(inverse[p][k : k + 1], SUB) * scale
            for q in range(p, panels):
                part = column[q][k] * scale
                if q == p:
                    part = jnp.where(level > k, part, 0.0)
                for j, head in enumerate(heads):
                    column[q][k + 1 + j] -= part * head
                upper[q] -= part * row
                inverse[q] -= part * back
            upper[p] = jnp.where(level == k, row, upper[p])
            inverse[p] = jnp.where(level == k, back, inverse[p])
    for p in range(panels):
        upper[p] = jnp.where(lane >= level + SUB * p, upper[p], 0.0)
        inverse[p] = jnp.where(lane <= level + SUB * p, inverse[p], 0.0)
    return upper, inverse


def basis_kernel(entries, gram_ref, sampled_ref, basis_ref, triangle_ref, inverse_ref):
    upper, inverse = factor(gram_ref[...] / entries)
    for p, rows in enumerate(upper):
        triangle_ref[SUB * p : SUB * (p + 1)] = rows
    for p, rows in enumerate(inverse):
        inverse_ref[SUB * p : SUB * (p + 1)] = rows
    for h in range(sampled_ref.shape[0]):
        basis_ref[h] = lax.dot_general(
            sampled_ref[h],
            inverse_ref[...],
            (((1,), (1,)), ((), ())),
            precision=lax.Precision.HIGHEST,
            preferred_element_type=F32,
        )


def basis_of(gram, sampled, entries):
    return pl.pallas_call(
        functools.partial(basis_kernel, entries),
        out_shape=[
            jax.ShapeDtypeStruct(sampled.shape, F32),
            jax.ShapeDtypeStruct(gram.shape, F32),
        ],
        in_specs=[VMEM, VMEM],
        out_specs=[VMEM, VMEM],
        scratch_shapes=[pltpu.VMEM(gram.shape, F32)],
        compiler_params=params(12),
    )(gram, sampled)


def body(sketch, inverse_blocks, couple_up, couple_down, strip_harmonics):
    count, rows, width = sketch.shape
    place = lax.axis_index("wall").astype(jnp.int32).reshape(1)
    (state,) = apply_inverse(place, inverse_blocks, sketch, False)
    for sweep in range(SWEEPS):
        own, before, after = couple(place, strip_harmonics, couple_up, couple_down, state)
        coupled = own
        if count == BAND:
            coupled = own + before.astype(F32) + after.astype(F32)
        else:
            coupled = coupled.at[:BAND].add(before.astype(F32))
            coupled = coupled.at[count - BAND :].add(after.astype(F32))
        rhs = (sketch.astype(F32) - coupled).astype(BF16)
        if sweep < SWEEPS - 1:
            (state,) = apply_inverse(place, inverse_blocks, rhs, False)
        else:
            sampled, gram = apply_inverse(place, inverse_blocks, rhs, True)
    entries = lax.axis_size("harm") * lax.axis_size("wall") * count * rows
    return tuple(basis_of(all_sum(gram), sampled, entries))


def solution(mesh):
    return jax.shard_map(
        body,
        mesh=mesh,
        in_specs=(
            P(("freq", "harm"), "wall", None),
            P(("freq", "harm"), "wall", None),
            P("freq", "wall", None),
            P("freq", "wall", None),
            P("freq"),
        ),
        out_specs=(P(("freq", "harm"), "wall", None), P("freq", None)),
        check_vma=False,
    )
```

```python
import functools

import jax
import jax.numpy as jnp
from jax import lax
from jax.experimental import pallas as pl
from jax.experimental.pallas import tpu as pltpu
from jax.sharding import PartitionSpec as P

BAND = 4
SWEEPS = 3
CHUNKS = 2
SUB = 8
F32 = jnp.float32
BF16 = jnp.bfloat16
VMEM = pl.BlockSpec(memory_space=pltpu.VMEM)
SMEM = pl.BlockSpec(memory_space=pltpu.SMEM)


def flip(value, axis, mask):
    return lax.ppermute(value, axis, [(i, i ^ mask) for i in range(lax.axis_size(axis))])


def turn(value, axis, step):
    count = lax.axis_size(axis)
    return lax.ppermute(value, axis, [(i, (i + step) % count) for i in range(count)])


def wall_pieces(own):
    pieces = {0: own}
    bit = lax.axis_size("wall") // 2
    while bit:
        for mask in list(pieces):
            pieces[mask ^ bit] = flip(pieces[mask], "wall", bit)
        bit //= 2
    return [pieces[mask] for mask in range(len(pieces))]


def params(mib):
    return pltpu.CompilerParams(vmem_limit_bytes=mib << 20)


def cost(flops, *arrays):
    moved = sum(a.size * a.dtype.itemsize for a in arrays)
    return pl.CostEstimate(flops=flops, bytes_accessed=moved, transcendentals=0)


def turned_dot(left, right, **how):
    return lax.dot_general(left, right, (((1,), (1,)), ((), ())), preferred_element_type=F32, **how)


def ordered(weights_ref, index, place, shards):
    rows = weights_ref.shape[2] // shards
    return jnp.concatenate(
        [
            weights_ref[index, :, pl.ds(pl.multiple_of((place ^ mask) * rows, rows), rows)]
            for mask in range(shards)
        ],
        axis=1,
    )


def split_kernel(sketch_ref, *chunk_refs):
    part = chunk_refs[0].shape[1]
    for h in range(sketch_ref.shape[0]):
        turned = sketch_ref[h].T
        for i, ref in enumerate(chunk_refs):
            ref[h] = turned[i * part : (i + 1) * part]


def split(sketch):
    count, rows, width = sketch.shape
    out = jax.ShapeDtypeStruct((count, width // CHUNKS, rows), BF16)
    return pl.pallas_call(
        split_kernel,
        out_shape=[out] * CHUNKS,
        in_specs=[VMEM],
        out_specs=[VMEM] * CHUNKS,
        compiler_params=params(4),
        cost_estimate=cost(0, sketch, sketch),
    )(sketch)


def inverse_kernel(shards, place_ref, blocks_ref, *refs):
    pieces, out_ref = refs[:shards], refs[shards]
    for h in range(out_ref.shape[0]):
        wide = jnp.concatenate([p[h] for p in pieces], axis=1)
        total = turned_dot(wide, ordered(blocks_ref, h, place_ref[0], shards))
        out_ref[h] = total.astype(out_ref.dtype)


def apply_inverse(place, blocks, source, dtype):
    pieces = wall_pieces(source)
    return pl.pallas_call(
        functools.partial(inverse_kernel, len(pieces)),
        out_shape=jax.ShapeDtypeStruct(source.shape, dtype),
        in_specs=[SMEM, VMEM] + [VMEM] * len(pieces),
        out_specs=VMEM,
        compiler_params=params(12),
        cost_estimate=cost(2 * blocks.size * source.shape[1], blocks, *pieces),
    )(place, blocks, *pieces)


def couple_kernel(shards, place_ref, strip_ref, up_ref, down_ref, *refs):
    pieces = refs[:shards]
    own_ref, below_ref, above_ref, total = refs[shards:]
    count, part, rows = pieces[0].shape
    total[...] = jnp.zeros_like(total)
    wide = jnp.concatenate([p[...].reshape(count * part, rows) for p in pieces], axis=1)
    for j in range(BAND):
        offset = strip_ref[j] + 1
        for weights, shift in ((up_ref, offset), (down_ref, -offset)):
            added = turned_dot(wide, ordered(weights, j, place_ref[0], shards))
            total[pl.ds(BAND + shift, count)] += added.reshape(count, part, rows)
    own_ref[...] = total[BAND : BAND + count]
    below_ref[...] = total[:BAND].astype(below_ref.dtype)
    above_ref[...] = total[BAND + count :].astype(above_ref.dtype)


def couple(place, strips, up, down, state):
    pieces = wall_pieces(state)
    count, part, rows = state.shape
    halo = jax.ShapeDtypeStruct((BAND, part, rows), BF16)
    own, below, above = pl.pallas_call(
        functools.partial(couple_kernel, len(pieces)),
        out_shape=[jax.ShapeDtypeStruct(state.shape, F32), halo, halo],
        in_specs=[SMEM, SMEM, VMEM, VMEM] + [VMEM] * len(pieces),
        out_specs=[VMEM] * 3,
        scratch_shapes=[pltpu.VMEM((count + 2 * BAND, part, rows), F32)],
        compiler_params=params(20),
        cost_estimate=cost(2 * (up.size + down.size) * count * part, up, down, *pieces),
    )(place, strips, up, down, *pieces)
    before = turn(above, "harm", 1).astype(F32)
    after = turn(below, "harm", -1).astype(F32)
    if count == BAND:
        return own + before + after
    return own.at[:BAND].add(before).at[count - BAND :].add(after)


def all_sum(value):
    for axis in ("wall", "harm"):
        bit = 1
        while bit < lax.axis_size(axis):
            value = value + flip(value, axis, bit)
            bit *= 2
    return value


def gram_kernel(*refs):
    chunks, gram_ref = refs[:-1], refs[-1]
    gram = jnp.zeros(gram_ref.shape, F32)
    for h in range(chunks[0].shape[0]):
        wide = jnp.concatenate([c[h] for c in chunks], axis=0)
        gram += turned_dot(wide, wide, precision=lax.Precision.HIGHEST)
    gram_ref[...] = gram


def gram_of(chunks):
    width = sum(c.shape[1] for c in chunks)
    return pl.pallas_call(
        gram_kernel,
        out_shape=jax.ShapeDtypeStruct((width, width), F32),
        in_specs=[VMEM] * len(chunks),
        out_specs=VMEM,
        compiler_params=params(8),
    )(*chunks)


def spread(row, height):
    return jnp.broadcast_to(row, (height, row.shape[1]))


def factor(gram):
    size = gram.shape[0]
    panels = size // SUB
    level = lax.broadcasted_iota(jnp.int32, (SUB, size), 0)
    lane = lax.broadcasted_iota(jnp.int32, (SUB, size), 1)
    upper = [gram[SUB * p : SUB * (p + 1)] for p in range(panels)]
    inverse = [jnp.where(lane == level + SUB * p, 1.0, 0.0) for p in range(panels)]
    for p in range(panels):
        column = {
            q: [
                jnp.broadcast_to(upper[q][:, SUB * p + j : SUB * p + j + 1], (SUB, size))
                for j in range(SUB)
            ]
            for q in range(p, panels)
        }
        for k in range(SUB):
            scale = lax.rsqrt(spread(column[p][k][k : k + 1], SUB))
            heads = [spread(column[p][j][k : k + 1], SUB) * scale for j in range(k + 1, SUB)]
            row = spread(upper[p][k : k + 1], SUB) * scale
            back = spread(inverse[p][k : k + 1], SUB) * scale
            for q in range(p, panels):
                part = column[q][k] * scale
                if q == p:
                    part = jnp.where(level > k, part, 0.0)
                for j, head in enumerate(heads):
                    column[q][k + 1 + j] -= part * head
                upper[q] -= part * row
                inverse[q] -= part * back
            upper[p] = jnp.where(level == k, row, upper[p])
            inverse[p] = jnp.where(level == k, back, inverse[p])
    for p in range(panels):
        upper[p] = jnp.where(lane >= level + SUB * p, upper[p], 0.0)
        inverse[p] = jnp.where(lane <= level + SUB * p, inverse[p], 0.0)
    return upper, inverse


def basis_kernel(entries, gram_ref, *refs):
    chunks = refs[:CHUNKS]
    basis_ref, triangle_ref, inverse_ref = refs[CHUNKS:]
    upper, inverse = factor(gram_ref[...] / entries)
    for p, rows in enumerate(upper):
        triangle_ref[SUB * p : SUB * (p + 1)] = rows
    for p, rows in enumerate(inverse):
        inverse_ref[SUB * p : SUB * (p + 1)] = rows
    for h in range(basis_ref.shape[0]):
        wide = jnp.concatenate([c[h] for c in chunks], axis=0)
        basis_ref[h] = jnp.dot(
            inverse_ref[...],
            wide,
            precision=lax.Precision.HIGHEST,
            preferred_element_type=F32,
        ).T


def basis_of(gram, chunks, shape, entries):
    return pl.pallas_call(
        functools.partial(basis_kernel, entries),
        out_shape=[jax.ShapeDtypeStruct(shape, F32), jax.ShapeDtypeStruct(gram.shape, F32)],
        in_specs=[VMEM] * (1 + CHUNKS),
        out_specs=[VMEM, VMEM],
        scratch_shapes=[pltpu.VMEM(gram.shape, F32)],
        compiler_params=params(12),
    )(gram, *chunks)


def body(sketch, inverse_blocks, couple_up, couple_down, strip_harmonics):
    count, rows, width = sketch.shape
    place = lax.axis_index("wall").astype(jnp.int32).reshape(1)
    sampled = []
    for chunk in split(sketch):
        state = apply_inverse(place, inverse_blocks, chunk, BF16)
        for sweep in range(SWEEPS):
            coupled = couple(place, strip_harmonics, couple_up, couple_down, state)
            rhs = (chunk.astype(F32) - coupled).astype(BF16)
            last = sweep == SWEEPS - 1
            state = apply_inverse(place, inverse_blocks, rhs, F32 if last else BF16)
        sampled.append(state)
    entries = lax.axis_size("harm") * lax.axis_size("wall") * count * rows
    gram = all_sum(gram_of(sampled))
    return tuple(basis_of(gram, sampled, sketch.shape, entries))


def solution(mesh):
    return jax.shard_map(
        body,
        mesh=mesh,
        in_specs=(
            P(("freq", "harm"), "wall", None),
            P(("freq", "harm"), "wall", None),
            P("freq", "wall", None),
            P("freq", "wall", None),
            P("freq"),
        ),
        out_specs=(P(("freq", "harm"), "wall", None), P("freq", None)),
        check_vma=False,
    )
```
